256 devices in a mesh: row: 16 (over z, x_hi), col: 16 (over y, x_lo, core).
Axes of the slice: x: 4 (x_hi: 2, x_lo: 2; x = x_hi * 2 + x_lo), y: 4, z: 8, core: 2. Of those that a mesh axis runs over, the one named last changes fastest.
Arguments:
- amplitudes: bfloat16 [8192, 8192], P('row', 'col'), may hold values from -6 to 6
- integrals: bfloat16 [8192, 8192], P('col', 'row'), may hold values from -0.09375 to 0.09375
- base_residual: float32 [8192, 8192], P('row', 'col'), may hold values from -6 to 6
- inv_denominators: float32 [8192, 8192], P('row', 'col'), may hold values from 0.1 to 0.5
- amp_mask: int32 [32, 32], P('row', 'col'), may hold values 0 or 1
- int_mask: int32 [32, 32], P('col', 'row'), may hold values 0 or 1
- res_mask: int32 [32, 32], P('row', 'col'), may hold values 0 or 1
Outputs:
- new_amplitudes: bfloat16 [8192, 8192], P('row', 'col')
- residual: float32 [8192, 8192], P('row', 'col')
The draws below stay inside these ranges and needn't reach their ends.
Inputs may be any that keep to these rules, and one draw needn't show every extreme that they name: `amp_mask`: tile kept (1) or dropped (0). `int_mask`: tile kept (1) or dropped (0). `res_mask`: tile kept (1) or dropped (0).
All inputs are finite; a program needn't handle non-finite values. No bound on the sum of `amp_mask` or of `int_mask` or of `res_mask` on one device may be relied on, other than what follows from the above.
Results may differ from the reference program's by a relative error of at most 0.012.
Values may be sent and summed in bfloat16 or wider, within the bound.
No kernel may reach another device: no remote copies, remote signals or barrier semaphores. Data moves between devices by JAX's collectives and lax.ppermute only.
A program may use at most 128 MiB of HBM per device.

```python
import math
import jax
import jax.numpy as jnp
from jax import lax

B = 256
ITERS = 2
NI = 8192
NK = 8192
N_COL = 16


def touch_ends(array, own_key, least, largest):
    longest = array.shape.index(max(array.shape))
    spots = []
    for shift in (0, 1):
        where = [jax.random.randint(jax.random.fold_in(own_key, axis), (), 0, length) for axis, length in enumerate(array.shape)]
        where[longest] = (where[longest] + shift) % array.shape[longest]
        spots.append(tuple(where))
    return array.at[spots[0]].set(least).at[spots[1]].set(largest)


def strengthened(values, own_key, source, target, parts, factor):
    def block_of(dim):
        return (jnp.arange(values.shape[dim]) // (values.shape[dim] // parts)).reshape((-1,) + (1,) * (values.ndim - 1 - dim))

    near = jax.random.permutation(own_key, parts)[block_of(target)]
    far = (block_of(target) + parts // 2) % parts
    return jnp.where((block_of(source) == near) | (block_of(source) == far), factor * values, values)


def block_levels(rng, dims, cuts, smallest, high):
    factor_of, own = 1.0, jax.random.fold_in(rng, 6)
    for dim, shards_of in cuts:
        steps = jnp.exp(jax.random.uniform(jax.random.fold_in(own, dim), (shards_of,), jnp.float32, smallest / len(cuts), high / len(cuts)))
        factor_of = factor_of * jnp.repeat(steps, dims[dim] // shards_of).reshape([-1 if axis == dim else 1 for axis in range(len(dims))])
    return factor_of


def bell_draw(rng, dims, scale, reach, pieces=(), kind=jnp.bfloat16):
    drawn = scale * jax.random.normal(rng, dims, jnp.float32)
    if pieces:
        drawn = drawn * block_levels(rng, dims, pieces, -0.22, 0.18)
    return jnp.clip(drawn, -reach, reach).astype(kind)


def heavy_noise(key, extent, spread, bound, split, heavy, held_as=jnp.bfloat16):
    drawn = spread * jax.random.normal(key, extent, jnp.float32)
    if split:
        drawn = drawn * block_levels(key, extent, split, -0.22, 0.18)
    return jnp.clip(strengthened(drawn, jax.random.fold_in(key, 3), *heavy), -bound, bound).astype(held_as)


def setup_inputs(seed: int = 0) -> dict:
    seeds = jax.random.split(jax.random.key(seed), 8)
    return {
        "amplitudes": bell_draw(seeds[0], (NI, NK), 1.0, 6.0, ((0, 16), (1, 16))),
        "integrals": heavy_noise(seeds[1], (NK, NK), NK ** -0.5, 0.09375, ((0, 16), (1, 16)), (0, 1, 16, 2.0)),
        "base_residual": bell_draw(seeds[2], (NI, NK), 1.0, 6.0, ((0, 16), (1, 16)), jnp.float32),
        "inv_denominators": jnp.clip(jnp.exp(math.log(0.5) - 1.609438 * jax.random.uniform(seeds[3], (NI, NK), jnp.float32) ** block_levels(seeds[3], (NI, NK), ((0, 16), (1, 16)), -0.2, 0.2)), 0.1, 0.5),
        "amp_mask": touch_ends((jax.random.randint(seeds[4], (NI // B, NK // B), 0, 4) < 3).astype(jnp.int32), jax.random.fold_in(seeds[4], 1), 0, 1),
        "int_mask": touch_ends((jax.random.randint(seeds[5], (NK // B, NK // B), 0, 4) < 3).astype(jnp.int32), jax.random.fold_in(seeds[5], 1), 0, 1),
        "res_mask": touch_ends((jax.random.randint(seeds[6], (NI // B, NK // B), 0, 4) < 3).astype(jnp.int32), jax.random.fold_in(seeds[6], 1), 0, 1),
    }


def expand(block, mask):
    tile_rows, tile_cols = mask.shape
    rows, cols = block.shape
    shaped = block.reshape(tile_rows, rows // tile_rows, tile_cols, cols // tile_cols)
    return (shaped * mask[:, None, :, None].astype(block.dtype)).reshape(rows, cols)


def reference(amplitudes, integrals, base_residual, inv_denominators, amp_mask, int_mask, res_mask):
    masked_ints = expand(integrals, int_mask)
    width = integrals.shape[0] // N_COL
    amps = amplitudes
    residual = base_residual
    for step in range(ITERS):
        masked_amps = expand(amps, amp_mask)

        def add_block(total, index):
            start = (index * width).astype(jnp.int32)
            left = lax.dynamic_slice_in_dim(masked_amps, start, width, 1)
            right = lax.dynamic_slice_in_dim(masked_ints, start, width, 0)
            part = jnp.dot(left, right, preferred_element_type=jnp.float32).astype(jnp.bfloat16)
            part = lax.optimization_barrier(part)
            return total + part.astype(jnp.float32), None

        start_total = jnp.zeros(base_residual.shape, jnp.float32)
        ladder, _ = lax.scan(add_block, start_total, jnp.arange(N_COL, dtype=jnp.int32))
        residual = expand(base_residual + ladder, res_mask)
        amps = (amps.astype(jnp.float32) - inv_denominators * residual).astype(jnp.bfloat16)
    return amps, residual
```

```python
import functools

import jax
import jax.numpy as jnp
from jax import lax
from jax.experimental import pallas as pl
from jax.experimental.pallas import tpu as pltpu
from jax.sharding import Mesh
from jax.sharding import PartitionSpec as P

AX = ("xh", "xl", "c")
BF = jnp.bfloat16
F32 = jnp.float32
CHUNKS = 2
LIMIT = 24 << 20
ROWS = 512 // CHUNKS
VM = pl.BlockSpec(memory_space=pltpu.VMEM)
SM = pl.BlockSpec(memory_space=pltpu.SMEM)
ANY = pl.BlockSpec(memory_space=pl.ANY)


def shape(*dims, dtype=BF):
    return jax.ShapeDtypeStruct(dims, dtype)


def permute_x(value, move):
    pairs = []
    for xh in range(2):
        for xl in range(2):
            for c in range(2):
                th, tl, tc = move(xh, xl, c)
                pairs.append((xh * 4 + xl * 2 + c, th * 4 + tl * 2 + tc))
    return lax.ppermute(value, AX, pairs)


def chip_xor(value, j):
    return permute_x(value, lambda xh, xl, c: (xh ^ (j >> 1), xl ^ (j & 1), c))


def core_swap(value):
    return permute_x(value, lambda xh, xl, c: (xh, xl, 1 - c))


def shift_z(value, s):
    return lax.ppermute(value, "z", [(i, (i + s) % 8) for i in range(8)])


def xor_y(value, t):
    return lax.ppermute(value, "y", [(i, i ^ t) for i in range(4)])


def call(body, outs, in_specs, out_specs, flops=0, moved=1 << 20, **kw):
    return pl.pallas_call(
        body,
        out_shape=outs,
        in_specs=in_specs,
        out_specs=out_specs,
        cost_estimate=pl.CostEstimate(flops=flops, bytes_accessed=moved, transcendentals=0),
        compiler_params=pltpu.CompilerParams(vmem_limit_bytes=LIMIT),
        **kw,
    )


def lanes(q):
    return pl.ds(pl.multiple_of(q * 128, 128), 128)


def prep_w(mask, ints, *outs):
    c, xl = lax.axis_index("c"), lax.axis_index("xl")
    for a in range(2):
        for b in range(2):
            col = c ^ a
            for r in range(2):
                keep = mask[r, col].astype(BF)
                outs[a * 2 + b][r * 256 : r * 256 + 256] = ints[r * 256 : r * 256 + 256, lanes(col * 2 + (xl ^ b))] * keep


def join_w(low, high, out):
    out[:512] = low[...]
    out[512:] = high[...]


def prep_a(idx, amask, rmask, amps, base, invd, masked, *outs):
    d = idx[0]
    for r in range(2):
        rows = slice(r * 256, r * 256 + 256)
        for s in range(2):
            cols = slice(s * 256, s * 256 + 256)
            masked[rows, cols] = amps[rows, cols] * amask[r, s].astype(BF)
        for j in range(4):
            q = d ^ j
            keep = (amask[r, q >> 1] * rmask[r, q >> 1]).astype(F32)
            outs[j][0, rows] = base[rows, lanes(q)].astype(BF)
            outs[j][1, rows] = (invd[rows, lanes(q)] * keep).astype(BF)


EVEN = ((0, 1), (6, 7), (2, 3), (4, 5))
ODD = ((7, 0), (1, 2), (5, 6), (3, 4))


def first_kernel(k, chunks, save, count, idx, *refs):
    even, odd, left = refs[:4], refs[4:8], refs[8:16]
    refs = refs[16 + count :]
    sends = refs[: 4 * len(chunks)]
    refs = refs[4 * len(chunks) :]
    if save:
        w_all, refs = refs[0], refs[1:]
    wv, outv, sem, wsem, osem = refs
    d, c, xh, xl, z, y = (idx[i] for i in range(6))
    odd_z = z & 1
    step = (0, 3 - odd_z * 2, 1 + odd_z * 2, 2)[k]
    dest = (z // 2 + step) & 3

    def loads(group):
        return [
            pltpu.make_async_copy(group[e * 2 + a], wv.at[a, :, pl.ds(e * 128, 128)], sem.at[e * 2 + a])
            for e in range(2)
            for a in range(2)
        ]

    @pl.when(odd_z == 0)
    def _():
        for copy in loads(even):
            copy.start()

    @pl.when(odd_z == 1)
    def _():
        for copy in loads(odd):
            copy.start()

    for copy in loads(even):
        copy.wait()

    flip = c ^ xh
    saves = []
    for g in range(2):
        for j in range(4):
            for e in range(2):
                row = pl.multiple_of((e ^ xl) * 512 + (d ^ j) * 128, 128)
                if save:
                    saves.append(
                        pltpu.make_async_copy(
                            wv.at[g ^ flip, pl.ds(row, 128)],
                            w_all.at[dest, pl.ds(((g * 4 + j) * 2 + e) * 128, 128)],
                            wsem.at[(g * 4 + j) * 2 + e],
                        )
                    )
    for copy in saves:
        copy.start()

    for half in range(2):
        own = jnp.concatenate([left[half * 2][...], left[half * 2 + 1][...]], 1)
        other = jnp.concatenate([left[4 + half * 2][...], left[4 + half * 2 + 1][...]], 1)
        total = jnp.dot(own, wv[flip], preferred_element_type=F32)
        total += jnp.dot(other, wv[1 - flip], preferred_element_type=F32)
        outv[xh ^ half] = total.astype(BF)

    def stores(t):
        return [
            pltpu.make_async_copy(outv.at[:, pl.ds(i * ROWS, ROWS)], sends[t * len(chunks) + i], osem.at[i])
            for i in range(len(chunks))
        ]

    for t in range(4):

        @pl.when((dest ^ y) == t)
        def _(t=t):
            for copy in stores(t):
                copy.start()

    for copy in stores(0):
        copy.wait()
    for copy in saves:
        copy.wait()


def first_product(k, idx, pieces, left, sends, w_all, chunks, save):
    group = [pieces[a][s] for s in EVEN[k] for a in range(2)] + [pieces[a][s] for s in ODD[k] for a in range(2)]
    outs = [shape(2, ROWS, 256)] * (4 * len(chunks)) + ([shape(4, 2048, 256)] if save else [])
    carried = [] if k == 0 else [sends[t][n] for t in range(4) for n in chunks] + ([w_all] if save else [])
    inputs = [idx] + group + left + carried
    rows = len(chunks) * ROWS
    block = pl.BlockSpec((rows, 512), lambda i: (chunks[0] if len(chunks) == 1 else 0, 0))
    got = call(
        functools.partial(first_kernel, k, chunks, save, len(carried)),
        outs,
        [SM] + [ANY] * 8 + [block] * 8 + [ANY] * len(carried),
        [ANY] * len(outs),
        flops=2 * 2 * rows * 2048 * 256,
        moved=6 << 20,
        grid=(1,),
        scratch_shapes=[
            pltpu.VMEM((2, 1024, 256), BF),
            pltpu.VMEM((2, rows, 256), BF),
            pltpu.SemaphoreType.DMA((4,)),
            pltpu.SemaphoreType.DMA((16,)),
            pltpu.SemaphoreType.DMA((CHUNKS,)),
        ],
        input_output_aliases={17 + i: i for i in range(len(carried))},
    )(*inputs)
    sends = [list(row) for row in sends] if sends else [[None] * CHUNKS for _ in range(4)]
    for t in range(4):
        for i, n in enumerate(chunks):
            sends[t][n] = got[t * len(chunks) + i]
    return sends, got[-1] if save else w_all


def second_kernel(order, dests, *refs):
    left, weights, outs = refs[:8], refs[8], refs[9:]
    whole = jnp.concatenate([ref[...].reshape(2 * ROWS, 256) for ref in left], 1)
    got = jnp.dot(whole, weights[...], preferred_element_type=F32).astype(BF).reshape(2, ROWS, 256)
    for i in range(len(order)):

        @pl.when(pl.program_id(0) == i)
        def _(i=i):
            outs[i][...] = got


def second_product(order, dests, left, w_all):
    whole = pl.BlockSpec((2, ROWS, 256), lambda i, s: (0, 0, 0))
    return pl.pallas_call(
        functools.partial(second_kernel, order),
        out_shape=[shape(2, ROWS, 256)] * len(order),
        grid_spec=pltpu.PrefetchScalarGridSpec(
            num_scalar_prefetch=1,
            grid=(len(order),),
            in_specs=[whole] * 8 + [pl.BlockSpec((None, 2048, 256), lambda i, s: (s[i], 0, 0))],
            out_specs=[whole] * len(order),
        ),
        name="second",
        compiler_params=pltpu.CompilerParams(vmem_limit_bytes=LIMIT),
        cost_estimate=pl.CostEstimate(
            flops=2 * 2 * ROWS * 2048 * 256 * len(order), bytes_accessed=(2 + len(order)) << 20, transcendentals=0
        ),
    )(dests, *left, w_all)


def update_kernel(idx, *refs):
    parts, left, terms, nxt, outs = refs[:4], refs[4:8], refs[8:12], refs[12], refs[13:]
    d = idx[0]
    for j in range(4):
        h, e = (d ^ j) >> 1, (d ^ j) & 1
        ladder = parts[0][h, :, lanes(e)].astype(F32)
        for part in parts[1:]:
            ladder += part[h, :, lanes(e)].astype(F32)
        outs[j][...] = ladder.astype(BF)
        step = terms[j][1].astype(F32) * (terms[j][0].astype(F32) + ladder)
        nxt[h, :, lanes(e)] = (left[j][...].astype(F32) - step).astype(BF)


def update(n, idx, parts, left, terms):
    whole = pl.BlockSpec((2, ROWS, 256), lambda i, s: (0, 0, 0))
    quarter = pl.BlockSpec((ROWS, 128), lambda i, s: (0, 0))
    return pl.pallas_call(
        update_kernel,
        out_shape=[shape(2, ROWS, 256)] + [shape(ROWS, 128)] * 4,
        grid_spec=pltpu.PrefetchScalarGridSpec(
            num_scalar_prefetch=1,
            grid=(1,),
            in_specs=[whole] * 4
            + [pl.BlockSpec((ROWS, 128), lambda i, s: (n, s[0]))] * 4
            + [pl.BlockSpec((2, ROWS, 128), lambda i, s: (0, n, 0))] * 4,
            out_specs=[whole] + [quarter] * 4,
        ),
        compiler_params=pltpu.CompilerParams(vmem_limit_bytes=LIMIT),
        cost_estimate=pl.CostEstimate(flops=0, bytes_accessed=2 << 20, transcendentals=0),
    )(idx, *parts, *left, *terms)


def sum_kernel(idx, *refs):
    parts, outs = refs[:4], refs[4:]
    d = idx[0]
    for j in range(4):
        h, e = (d ^ j) >> 1, (d ^ j) & 1
        ladder = parts[0][h, :, lanes(e)].astype(F32)
        for part in parts[1:]:
            ladder += part[h, :, lanes(e)].astype(F32)
        outs[j][...] = ladder.astype(BF)


def final_kernel(idx, mask, amps, base, invd, *refs):
    first, second, new, res = refs[: 4 * CHUNKS], refs[4 * CHUNKS : 8 * CHUNKS], refs[-2], refs[-1]
    d = idx[0]
    for n in range(CHUNKS):
        rows = slice(n * ROWS, (n + 1) * ROWS)
        for j in range(4):
            q = d ^ j
            keep = mask[n * ROWS // 256, q >> 1].astype(F32)
            fixed, inverse = base[rows, lanes(q)], invd[rows, lanes(q)]
            one = (fixed + first[n * 4 + j][...].astype(F32)) * keep
            mid = (amps[rows, lanes(q)].astype(F32) - inverse * one).astype(BF).astype(F32)
            two = (fixed + second[n * 4 + j][...].astype(F32)) * keep
            res[rows, lanes(q)] = two
            new[rows, lanes(q)] = (mid - inverse * two).astype(BF)


def after(value, *others):
    return lax.optimization_barrier((value, *others))[0]


def compute(amps, ints, base, invd, am, im, rm):
    z, y = lax.axis_index("z"), lax.axis_index("y")
    xh, xl, c = lax.axis_index("xh"), lax.axis_index("xl"), lax.axis_index("c")
    idx = jnp.stack([xh * 2 + xl, c, xh, xl, z, y]).astype(jnp.int32)

    cut = call(prep_w, [shape(512, 128)] * 4, [SM, VM], [VM] * 4)(im, ints)
    cut = [permute_x(v, lambda h, l, k, i=i: (k ^ (i >> 1), l ^ (i & 1), h)) for i, v in enumerate(cut)]
    own = [call(join_w, shape(1024, 128), [VM] * 2, VM)(cut[2 * a], cut[2 * a + 1]) for a in range(2)]

    masked, *terms = call(
        prep_a, [shape(512, 512)] + [shape(2, 512, 128)] * 4, [SM] * 3 + [VM] * 3, [VM] * 5, moved=4 << 20
    )(idx, am, rm, amps, base, invd)

    pieces = [[own[0]] + [None] * 7, [own[1]] + [None] * 7]
    up, down = list(own), list(own)
    for step in range(1, 4):
        for g in range(2):
            up[g] = shift_z(up[g], 1)
            down[g] = shift_z(down[g], -1)
            pieces[g][8 - step] = up[g]
            pieces[g][step] = down[g]
    pieces[0][4] = shift_z(up[0], 1)
    pieces[1][4] = shift_z(down[1], -1)

    held = after(masked, *own)
    left = [masked] + [chip_xor(held, j) for j in range(1, 4)]
    left = left + [core_swap(v) for v in left]
    terms = [terms[0]] + [chip_xor(after(terms[j], *left[1:4]), j) for j in range(1, 4)]

    sends, w_all = None, None
    for k in range(3):
        sends, w_all = first_product(k, idx, pieces, left, sends, w_all, (0, 1), True)
    sends, _ = first_product(3, idx, pieces, left, sends, w_all, (0,), False)
    sends, w_all = first_product(3, idx, pieces, left, sends, w_all, (1,), True)

    def reduced(sends):
        return [sends[0], *(xor_y(sends[t], t) for t in (2, 1, 3))]

    first, second = [], []
    for n in range(CHUNKS):
        nxt, *ladder = update(n, idx, reduced([sends[t][n] for t in range(4)]), left[:4], terms)
        first += [ladder[0]] + [chip_xor(ladder[j], j) for j in range(1, 4)]
        chips = [nxt] + [chip_xor(nxt, j) for j in range(1, 4)]
        chips = chips + [core_swap(v) for v in chips]
        ladder = [None] * 4
        for order in ((2, 1), (3, 0)):
            got = second_product(order, jnp.stack([y ^ t for t in order]).astype(jnp.int32), chips, w_all)
            for i, t in enumerate(order):
                ladder[t] = got[i]
        ladder = call(sum_kernel, [shape(ROWS, 128)] * 4, [SM] + [VM] * 4, [VM] * 4)(idx, *reduced(ladder))
        second += [ladder[0]] + [chip_xor(ladder[j], j) for j in range(1, 4)]
    return call(
        final_kernel,
        [shape(512, 512), shape(512, 512, dtype=F32)],
        [SM, SM] + [VM] * (3 + 8 * CHUNKS),
        [VM] * 2,
        moved=6 << 20,
    )(idx, rm, amps, base, invd, *first, *second)


def solution(mesh):
    split = Mesh(mesh.devices.reshape(8, 2, 4, 2, 2), ("z", "xh", "y", "xl", "c"))
    row, col = ("z", "xh"), ("y", "xl", "c")
    return jax.shard_map(
        compute,
        mesh=split,
        in_specs=(P(row, col), P(col, row), P(row, col), P(row, col), P(row, col), P(col, row), P(row, col)),
        out_specs=(P(row, col), P(row, col)),
        check_vma=False,
    )
```

```python
import functools

import jax
import jax.numpy as jnp
from jax import lax
from jax.experimental import pallas as pl
from jax.experimental.pallas import tpu as pltpu
from jax.sharding import Mesh
from jax.sharding import PartitionSpec as P

AX = ("xh", "xl", "c")
BF = jnp.bfloat16
F32 = jnp.float32
CHUNKS = 1
LIMIT = 24 << 20
ROWS = 512 // CHUNKS
VM = pl.BlockSpec(memory_space=pltpu.VMEM)
SM = pl.BlockSpec(memory_space=pltpu.SMEM)
ANY = pl.BlockSpec(memory_space=pl.ANY)


def shape(*dims, dtype=BF):
    return jax.ShapeDtypeStruct(dims, dtype)


def permute_x(value, move):
    pairs = []
    for xh in range(2):
        for xl in range(2):
            for c in range(2):
                th, tl, tc = move(xh, xl, c)
                pairs.append((xh * 4 + xl * 2 + c, th * 4 + tl * 2 + tc))
    return lax.ppermute(value, AX, pairs)


def chip_xor(value, j):
    return permute_x(value, lambda xh, xl, c: (xh ^ (j >> 1), xl ^ (j & 1), c))


def core_swap(value):
    return permute_x(value, lambda xh, xl, c: (xh, xl, 1 - c))


def shift_z(value, s):
    return lax.ppermute(value, "z", [(i, (i + s) % 8) for i in range(8)])


def xor_y(value, t):
    return lax.ppermute(value, "y", [(i, i ^ t) for i in range(4)])


def call(body, outs, in_specs, out_specs, flops=0, moved=1 << 20, **kw):
    return pl.pallas_call(
        body,
        out_shape=outs,
        in_specs=in_specs,
        out_specs=out_specs,
        cost_estimate=pl.CostEstimate(flops=flops, bytes_accessed=moved, transcendentals=0),
        compiler_params=pltpu.CompilerParams(vmem_limit_bytes=LIMIT),
        **kw,
    )


def kept(idx, which, r, s):
    return (idx[r, s] >> which) & 1


def placed(idx):
    place = idx[0, 0] >> 3
    return [(place >> at) & size for at, size in ((0, 3), (2, 1), (1, 1), (0, 1), (3, 7), (6, 3))]


AMASK, IMASK, RMASK = 0, 1, 2


def lanes(q):
    return pl.ds(pl.multiple_of(q * 128, 128), 128)


def prep_w(idx, ints, *outs):
    _, c, _, xl, _, _ = placed(idx)
    for a in range(2):
        for b in range(2):
            col = c ^ a
            for r in range(2):
                keep = kept(idx, IMASK, r, col).astype(BF)
                outs[a * 2 + b][r * 256 : r * 256 + 256] = ints[r * 256 : r * 256 + 256, lanes(col * 2 + (xl ^ b))] * keep


def join_w(low, high, out):
    out[:512] = low[...]
    out[512:] = high[...]


def join_a(one, two, three, out):
    out[0] = one[...]
    out[1] = two[...]
    out[2] = three[...]


def prep_a(idx, amps, masked):
    for r in range(2):
        for s in range(2):
            tile = (slice(r * 256, r * 256 + 256), slice(s * 256, s * 256 + 256))
            masked[tile] = amps[tile] * kept(idx, AMASK, r, s).astype(BF)


def prep_t(idx, base, invd, *outs):
    d = placed(idx)[0]
    for r in range(2):
        rows = slice(r * 256, r * 256 + 256)
        for j in range(4):
            q = d ^ j
            keep = (kept(idx, AMASK, r, q >> 1) * kept(idx, RMASK, r, q >> 1)).astype(F32)
            outs[j][0, rows] = base[rows, lanes(q)].astype(BF)
            outs[j][1, rows] = (invd[rows, lanes(q)] * keep).astype(BF)


EVEN = ((0, 1), (6, 7), (2, 3), (4, 5))
ODD = ((7, 0), (1, 2), (5, 6), (3, 4))


def first_kernel(ks, count, idx, *refs):
    pairs = [refs[8 * i : 8 * i + 8] for i in range(len(ks))]
    refs = refs[8 * len(ks) :]
    left, rest = refs[:5], refs[5]
    sends, wv, outv, osem = (lambda r: (r[:4], *r[4:]))(refs[6 + count :])
    _, c, xh, _, z, y = placed(idx)
    odd_z = z & 1
    flip = c ^ xh
    dests = [(z // 2 + (0, 3 - odd_z * 2, 1 + odd_z * 2, 2)[k]) & 3 for k in ks]

    def store(i, t):
        return pltpu.make_async_copy(outv.at[i], sends[t], osem.at[i])

    for i in range(len(ks)):
        for odd in range(2):

            @pl.when(odd_z == odd)
            def _(i=i, odd=odd):
                for e in range(2):
                    for a in range(2):
                        wv[a, :, e * 128 : e * 128 + 128] = pairs[i][odd * 4 + e * 2 + a][...]

        for half in range(2):
            own = jnp.concatenate([left[half * 2][...], left[half * 2 + 1][...]], 1)
            other = [left[4][...] if half == 0 else rest[1], rest[2 * half]]
            total = jnp.dot(own, wv[flip], preferred_element_type=F32)
            total += jnp.dot(jnp.concatenate(other, 1), wv[1 - flip], preferred_element_type=F32)
            outv[i, xh ^ half] = total.astype(BF)
        for t in range(4):

            @pl.when((dests[i] ^ y) == t)
            def _(i=i, t=t):
                store(i, t).start()

    for i in range(len(ks)):
        store(i, 0).wait()


def first_product(ks, idx, pieces, left, carried):
    group = [pieces[a][s] for k in ks for pairs in (EVEN[k], ODD[k]) for s in pairs for a in range(2)]
    return call(
        functools.partial(first_kernel, ks, len(carried)),
        [shape(2, 512, 256)] * 4,
        [SM] + [VM] * len(group) + [VM] * 6 + [ANY] * len(carried),
        [ANY] * 4,
        flops=len(ks) * 2 * 1024 * 2048 * 256,
        moved=len(ks) << 20,
        scratch_shapes=[
            pltpu.VMEM((2, 1024, 256), BF),
            pltpu.VMEM((len(ks), 2, 512, 256), BF),
            pltpu.SemaphoreType.DMA((len(ks),)),
        ],
        input_output_aliases={7 + len(group) + i: i for i in range(len(carried))},
    )(idx, *group, *left, *carried)


def arrange(idx, *refs):
    d, c, xh, xl, z, _ = placed(idx)
    out = refs[16]
    for a in range(2):
        for s in range(8):
            piece = refs[a * 8 + s]
            owner = (z + s) & 7

            @pl.loop(0, 8)
            def _(block, a=a, piece=piece, owner=owner):
                e, q = block >> 2, block & 3
                at = (((a ^ c ^ xh) * 4 + (q ^ d)) * 2 + (e ^ xl)) * 128
                rows = pl.ds(pl.multiple_of(at, 128), 128)
                out[owner >> 1, rows, lanes(owner & 1)] = piece[pl.ds(pl.multiple_of(block * 128, 128), 128)]


def second_kernel(order, idx, *refs):
    left, weights, outs = refs[:8], refs[8], refs[9:]

    @pl.loop(0, 2)
    def _(h):
        whole = jnp.concatenate([ref[h] for ref in left], 1)
        got = jnp.dot(whole, weights[...], preferred_element_type=F32).astype(BF)
        for i in range(len(order)):

            @pl.when(pl.program_id(0) == i)
            def _(i=i):
                outs[i][h] = got


def second_product(t, idx, left, w_all):
    order = (t,)
    whole = pl.BlockSpec((2, ROWS, 256), lambda i, s: (0, 0, 0))
    return pl.pallas_call(
        functools.partial(second_kernel, order),
        out_shape=[shape(2, ROWS, 256)] * len(order),
        grid_spec=pltpu.PrefetchScalarGridSpec(
            num_scalar_prefetch=1,
            grid=(len(order),),
            in_specs=[whole] * 8 + [pl.BlockSpec((None, 2048, 256), lambda i, s: (placed(s)[5] ^ t, 0, 0))],
            out_specs=[whole] * len(order),
        ),
        name="second",
        compiler_params=pltpu.CompilerParams(vmem_limit_bytes=LIMIT),
        cost_estimate=pl.CostEstimate(
            flops=2 * 2 * ROWS * 2048 * 256 * len(order), bytes_accessed=(2 + len(order)) << 20, transcendentals=0
        ),
    )(idx, *left, w_all)[0]


def update_kernel(idx, *refs):
    parts, left, terms, nxt, outs = refs[:4], refs[4:8], refs[8:12], refs[-5], refs[-4:]
    d = placed(idx)[0]
    for j in range(4):
        h, e = (d ^ j) >> 1, (d ^ j) & 1
        ladder = parts[0][h, :, lanes(e)].astype(F32)
        for part in parts[1:]:
            ladder += part[h, :, lanes(e)].astype(F32)
        outs[j][...] = ladder.astype(BF)
        step = terms[j][1].astype(F32) * (terms[j][0].astype(F32) + ladder)
        nxt[h, :, lanes(e)] = (left[j][...].astype(F32) - step).astype(BF)


def update(n, idx, parts, left, terms, carried):
    whole = pl.BlockSpec((2, ROWS, 256), lambda i, s: (0, 0, 0))
    quarter = pl.BlockSpec((ROWS, 128), lambda i, s: (n, 0))
    return pl.pallas_call(
        update_kernel,
        out_shape=[shape(2, ROWS, 256)] + [shape(512, 128)] * 4,
        grid_spec=pltpu.PrefetchScalarGridSpec(
            num_scalar_prefetch=1,
            grid=(1,),
            in_specs=[whole] * 4
            + [pl.BlockSpec((ROWS, 128), lambda i, s: (n, placed(s)[0]))] * 4
            + [pl.BlockSpec((2, ROWS, 128), lambda i, s: (0, n, 0))] * 4
            + [ANY] * len(carried),
            out_specs=[whole] + [quarter] * 4,
        ),
        compiler_params=pltpu.CompilerParams(vmem_limit_bytes=LIMIT),
        cost_estimate=pl.CostEstimate(flops=0, bytes_accessed=2 << 20, transcendentals=0),
        input_output_aliases={13 + i: 1 + i for i in range(len(carried))},
    )(idx, *parts, *left, *terms, *carried)


def sum_kernel(idx, *refs):
    parts, outs = refs[:-4], refs[-4:]
    d = placed(idx)[0]
    for n in range(CHUNKS):
        for j in range(4):
            h, e = (d ^ j) >> 1, (d ^ j) & 1
            ladder = parts[n * 4][h, :, lanes(e)].astype(F32)
            for part in parts[n * 4 + 1 : n * 4 + 4]:
                ladder += part[h, :, lanes(e)].astype(F32)
            outs[j][n * ROWS : (n + 1) * ROWS] = ladder.astype(BF)


def final_kernel(idx, amps, base, invd, *refs):
    first, second, new, res = refs[:4], refs[4:8], refs[-2], refs[-1]
    d = placed(idx)[0]
    for r in range(2):
        rows = slice(r * 256, r * 256 + 256)
        for j in range(4):
            q = d ^ j
            keep = kept(idx, RMASK, r, q >> 1).astype(F32)
            fixed, inverse = base[rows, lanes(q)], invd[rows, lanes(q)]
            one = (fixed + first[j][rows].astype(F32)) * keep
            mid = (amps[rows, lanes(q)].astype(F32) - inverse * one).astype(BF).astype(F32)
            two = (fixed + second[j][rows].astype(F32)) * keep
            res[rows, lanes(q)] = two
            new[rows, lanes(q)] = (mid - inverse * two).astype(BF)


def compute(amps, ints, base, invd, am, im, rm):
    z, y = lax.axis_index("z"), lax.axis_index("y")
    xh, xl, c = lax.axis_index("xh"), lax.axis_index("xl"), lax.axis_index("c")
    place = (xh * 2 + xl) | (c << 2) | (z << 3) | (y << 6)
    idx = (am | (im << IMASK) | (rm << RMASK) | (place << 3)).astype(jnp.int32)

    cut = list(call(prep_w, [shape(512, 128)] * 4, [SM, VM], [VM] * 4)(idx, ints))
    for i in range(4):
        cut[i] = permute_x(cut[i], lambda h, l, k, i=i: (k ^ (i >> 1), l ^ (i & 1), h))
    own = [call(join_w, shape(1024, 128), [VM] * 2, VM)(cut[2 * a], cut[2 * a + 1]) for a in range(2)]

    masked = call(prep_a, shape(512, 512), [SM, VM], VM)(idx, amps)
    terms = call(prep_t, [shape(2, 512, 128)] * 4, [SM, VM, VM], [VM] * 4)(idx, base, invd)

    pieces = [[own[0]] + [None] * 7, [own[1]] + [None] * 7]
    up, down = list(own), list(own)
    for step in range(1, 4):
        for g in range(2):
            up[g] = shift_z(up[g], 1)
            down[g] = shift_z(down[g], -1)
            pieces[g][8 - step] = up[g]
            pieces[g][step] = down[g]
    pieces[0][4] = shift_z(up[0], 1)
    pieces[1][4] = shift_z(down[1], -1)

    left = [masked]
    for j in range(1, 4):
        left.append(chip_xor(masked, j))
    left.append(core_swap(masked))
    joined = call(join_a, shape(3, 512, 512), [VM] * 3, VM)(*left[1:4])
    left.append(core_swap(joined))
    terms = list(terms)
    for j in range(1, 4):
        terms[j] = chip_xor(terms[j], j)

    sends = first_product((0, 1), idx, pieces, left, [])
    sends = first_product((2,), idx, pieces, left, sends)
    sends = first_product((3,), idx, pieces, left, sends)
    w_all = call(arrange, shape(4, 2048, 256), [SM] + [VM] * 16, VM, moved=8 << 20)(idx, *pieces[0], *pieces[1])

    def reduced(sends):
        got = [sends[0]] + [None] * 3
        for t in (2, 1, 3):
            got[t] = xor_y(sends[t], t)
        return got

    def spread(values):
        got = [values[0]] + [None] * 3
        for j in (2, 1, 3):
            got[j] = chip_xor(values[j], j)
        return got

    nxt, *ladder = update(0, idx, reduced(sends), left[:4], terms, [])
    chips = spread([nxt] * 4)
    chips = chips + [core_swap(v) for v in chips]
    parts = [None] * 4
    for t in (2, 1, 3, 0):
        parts[t] = second_product(t, idx, chips, w_all)
    parts = reduced(parts)
    first = spread(ladder)
    ladder = call(sum_kernel, [shape(512, 128)] * 4, [SM] + [VM] * 4, [VM] * 4)(idx, *parts)
    second = spread(ladder)
    return call(
        final_kernel, [shape(512, 512), shape(512, 512, dtype=F32)], [SM] + [VM] * 11, [VM] * 2, moved=6 << 20
    )(idx, amps, base, invd, *first, *second)


def solution(mesh):
    split = Mesh(mesh.devices.reshape(8, 2, 4, 2, 2), ("z", "xh", "y", "xl", "c"))
    row, col = ("z", "xh"), ("y", "xl", "c")
    return jax.shard_map(
        compute,
        mesh=split,
        in_specs=(P(row, col), P(col, row), P(row, col), P(row, col), P(row, col), P(col, row), P(row, col)),
        out_specs=(P(row, col), P(row, col)),
        check_vma=False,
    )
```

```python
import functools

import jax
import jax.numpy as jnp
from jax import lax
from jax.experimental import pallas as pl
from jax.experimental.pallas import tpu as pltpu
from jax.sharding import Mesh
from jax.sharding import PartitionSpec as P

AX = ("xh", "xl", "c")
BF = jnp.bfloat16
F32 = jnp.float32
LIMIT = 24 << 20
ROWS = 512
VM = pl.BlockSpec(memory_space=pltpu.VMEM)
SM = pl.BlockSpec(memory_space=pltpu.SMEM)
ANY = pl.BlockSpec(memory_space=pl.ANY)


def shape(*dims, dtype=BF):
    return jax.ShapeDtypeStruct(dims, dtype)


def permute_x(value, move):
    pairs = []
    for xh in range(2):
        for xl in range(2):
            for c in range(2):
                th, tl, tc = move(xh, xl, c)
                pairs.append((xh * 4 + xl * 2 + c, th * 4 + tl * 2 + tc))
    return lax.ppermute(value, AX, pairs)


def chip_xor(value, j):
    return permute_x(value, lambda xh, xl, c: (xh ^ (j >> 1), xl ^ (j & 1), c))


def core_swap(value):
    return permute_x(value, lambda xh, xl, c: (xh, xl, 1 - c))


def shift_z(value, s):
    return lax.ppermute(value, "z", [(i, (i + s) % 8) for i in range(8)])


def xor_y(value, t):
    return lax.ppermute(value, "y", [(i, i ^ t) for i in range(4)])


def call(body, outs, in_specs, out_specs, flops=0, moved=1 << 20, **kw):
    return pl.pallas_call(
        body,
        out_shape=outs,
        in_specs=in_specs,
        out_specs=out_specs,
        cost_estimate=pl.CostEstimate(flops=flops, bytes_accessed=moved, transcendentals=0),
        compiler_params=pltpu.CompilerParams(vmem_limit_bytes=LIMIT),
        **kw,
    )


def kept(idx, which, r, s):
    return (idx[r, s] >> which) & 1


def placed(idx):
    place = idx[0, 0] >> 3
    return [(place >> at) & size for at, size in ((0, 3), (2, 1), (1, 1), (0, 1), (3, 7), (6, 3))]


AMASK, IMASK, RMASK = 0, 1, 2


def lanes(q):
    return pl.ds(pl.multiple_of(q * 128, 128), 128)


def prep_w(idx, ints, *outs):
    _, c, _, xl, _, _ = placed(idx)
    for a in range(2):
        for b in range(2):
            col = c ^ a
            for r in range(2):
                keep = kept(idx, IMASK, r, col).astype(BF)
                outs[a * 2 + b][r * 256 : r * 256 + 256] = ints[r * 256 : r * 256 + 256, lanes(col * 2 + (xl ^ b))] * keep


def join_w(low, high, out):
    out[:512] = low[...]
    out[512:] = high[...]


def join_a(zero, one, two, three, out):
    out[0] = zero[...]
    out[1] = one[...]
    out[2] = two[...]
    out[3] = three[...]


def prep_a(idx, amps, masked):
    for r in range(2):
        for s in range(2):
            tile = (slice(r * 256, r * 256 + 256), slice(s * 256, s * 256 + 256))
            masked[tile] = amps[tile] * kept(idx, AMASK, r, s).astype(BF)


def prep_t(idx, base, invd, *outs):
    d = placed(idx)[0]
    for r in range(2):
        rows = slice(r * 256, r * 256 + 256)
        for j in range(4):
            q = d ^ j
            keep = (kept(idx, AMASK, r, q >> 1) * kept(idx, RMASK, r, q >> 1)).astype(F32)
            outs[j][0, rows] = base[rows, lanes(q)].astype(BF)
            outs[j][1, rows] = (invd[rows, lanes(q)] * keep).astype(BF)


EVEN = ((0, 1), (6, 7), (2, 3), (4, 5))
ODD = ((7, 0), (1, 2), (5, 6), (3, 4))


def first_kernel(ks, count, idx, *refs):
    pairs = [refs[8 * i : 8 * i + 8] for i in range(len(ks))]
    refs = refs[8 * len(ks) :]
    left, rest = refs[:4], refs[4]
    sends, wv, outv, osem = (lambda r: (r[:4], *r[4:]))(refs[5 + count :])
    _, c, xh, _, z, y = placed(idx)
    odd_z = z & 1
    flip = c ^ xh
    dests = [(z // 2 + (0, 3 - odd_z * 2, 1 + odd_z * 2, 2)[k]) & 3 for k in ks]

    def store(i, t):
        return pltpu.make_async_copy(outv.at[i], sends[t], osem.at[i])

    for i in range(len(ks)):
        for odd in range(2):

            @pl.when(odd_z == odd)
            def _(i=i, odd=odd):
                for e in range(2):
                    for a in range(2):
                        wv[a, :, e * 128 : e * 128 + 128] = pairs[i][odd * 4 + e * 2 + a][...]

        for half in range(2):
            own = jnp.concatenate([left[half * 2][...], left[half * 2 + 1][...]], 1)
            other = jnp.concatenate([rest[half * 2], rest[half * 2 + 1]], 1)
            total = jnp.dot(own, wv[flip], preferred_element_type=F32)
            total += jnp.dot(other, wv[1 - flip], preferred_element_type=F32)
            outv[i, xh ^ half] = total.astype(BF)
        for t in range(4):

            @pl.when((dests[i] ^ y) == t)
            def _(i=i, t=t):
                store(i, t).start()

    for i in range(len(ks)):
        store(i, 0).wait()


def first_product(ks, idx, pieces, left, carried):
    group = [pieces[a][s] for k in ks for pairs in (EVEN[k], ODD[k]) for s in pairs for a in range(2)]
    return call(
        functools.partial(first_kernel, ks, len(carried)),
        [shape(2, 512, 256)] * 4,
        [SM] + [VM] * len(group) + [VM] * 5 + [ANY] * len(carried),
        [ANY] * 4,
        flops=len(ks) * 2 * 1024 * 2048 * 256,
        moved=len(ks) << 20,
        scratch_shapes=[
            pltpu.VMEM((2, 1024, 256), BF),
            pltpu.VMEM((len(ks), 2, 512, 256), BF),
            pltpu.SemaphoreType.DMA((len(ks),)),
        ],
        input_output_aliases={6 + len(group) + i: i for i in range(len(carried))},
    )(idx, *group, *left, *carried)


def arrange(idx, *refs):
    d, c, xh, xl, z, _ = placed(idx)
    out = refs[16]
    for a in range(2):
        for s in range(8):
            piece = refs[a * 8 + s]
            owner = (z + s) & 7

            @pl.loop(0, 8)
            def _(block, a=a, piece=piece, owner=owner):
                e, q = block >> 2, block & 3
                at = (((a ^ c ^ xh) * 4 + (q ^ d)) * 2 + (e ^ xl)) * 128
                rows = pl.ds(pl.multiple_of(at, 128), 128)
                out[owner >> 1, rows, lanes(owner & 1)] = piece[pl.ds(pl.multiple_of(block * 128, 128), 128)]


def second_kernel(order, idx, *refs):
    left, weights, outs = refs[:8], refs[8], refs[9:]

    @pl.loop(0, 2)
    def _(h):
        whole = jnp.concatenate([ref[h] for ref in left], 1)
        got = jnp.dot(whole, weights[...], preferred_element_type=F32).astype(BF)
        for i in range(len(order)):

            @pl.when(pl.program_id(0) == i)
            def _(i=i):
                outs[i][h] = got


def second_product(t, idx, left, w_all):
    order = (t,)
    whole = pl.BlockSpec((2, ROWS, 256), lambda i, s: (0, 0, 0))
    return pl.pallas_call(
        functools.partial(second_kernel, order),
        out_shape=[shape(2, ROWS, 256)] * len(order),
        grid_spec=pltpu.PrefetchScalarGridSpec(
            num_scalar_prefetch=1,
            grid=(len(order),),
            in_specs=[whole] * 8 + [pl.BlockSpec((None, 2048, 256), lambda i, s: (placed(s)[5] ^ t, 0, 0))],
            out_specs=[whole] * len(order),
        ),
        name="second",
        compiler_params=pltpu.CompilerParams(vmem_limit_bytes=LIMIT),
        cost_estimate=pl.CostEstimate(
            flops=2 * 2 * ROWS * 2048 * 256 * len(order), bytes_accessed=(2 + len(order)) << 20, transcendentals=0
        ),
    )(idx, *left, w_all)[0]


def summed(parts, h, e, rows):
    total = parts[0][h, rows, lanes(e)].astype(F32)
    for part in parts[1:]:
        total += part[h, rows, lanes(e)].astype(F32)
    return total


def update_kernel(idx, *refs):
    parts, left, terms, nxt, outs = refs[:4], refs[4:8], refs[8:12], refs[-5], refs[-4:]
    d = placed(idx)[0]

    @pl.loop(0, 4)
    def _(i):
        rows = lanes(i)
        for j in range(4):
            h, e = (d ^ j) >> 1, (d ^ j) & 1
            ladder = summed(parts, h, e, rows)
            outs[j][rows] = ladder.astype(BF)
            step = terms[j][1, rows].astype(F32) * (terms[j][0, rows].astype(F32) + ladder)
            nxt[h, rows, lanes(e)] = (left[j][rows].astype(F32) - step).astype(BF)


def update(n, idx, parts, left, terms, carried):
    whole = pl.BlockSpec((2, ROWS, 256), lambda i, s: (0, 0, 0))
    quarter = pl.BlockSpec((ROWS, 128), lambda i, s: (n, 0))
    return pl.pallas_call(
        update_kernel,
        out_shape=[shape(2, ROWS, 256)] + [shape(512, 128)] * 4,
        grid_spec=pltpu.PrefetchScalarGridSpec(
            num_scalar_prefetch=1,
            grid=(1,),
            in_specs=[whole] * 4
            + [pl.BlockSpec((ROWS, 128), lambda i, s: (n, placed(s)[0]))] * 4
            + [pl.BlockSpec((2, ROWS, 128), lambda i, s: (0, n, 0))] * 4
            + [ANY] * len(carried),
            out_specs=[whole] + [quarter] * 4,
        ),
        compiler_params=pltpu.CompilerParams(vmem_limit_bytes=LIMIT),
        cost_estimate=pl.CostEstimate(flops=0, bytes_accessed=2 << 20, transcendentals=0),
        input_output_aliases={13 + i: 1 + i for i in range(len(carried))},
    )(idx, *parts, *left, *terms, *carried)


def sum_kernel(idx, *refs):
    parts, outs = refs[:-4], refs[-4:]
    d = placed(idx)[0]

    @pl.loop(0, 4)
    def _(i):
        rows = lanes(i)
        for j in range(4):
            outs[j][rows] = summed(parts, (d ^ j) >> 1, (d ^ j) & 1, rows).astype(BF)


def final_kernel(idx, amps, base, invd, *refs):
    first, second, new, res = refs[:4], refs[4:8], refs[-2], refs[-1]
    d = placed(idx)[0]

    @pl.loop(0, 4)
    def _(i):
        rows = lanes(i)
        for j in range(4):
            q = d ^ j
            keep = kept(idx, RMASK, i >> 1, q >> 1).astype(F32)
            fixed, inverse = base[rows, lanes(q)], invd[rows, lanes(q)]
            one = (fixed + first[j][rows].astype(F32)) * keep
            mid = (amps[rows, lanes(q)].astype(F32) - inverse * one).astype(BF).astype(F32)
            two = (fixed + second[j][rows].astype(F32)) * keep
            res[rows, lanes(q)] = two
            new[rows, lanes(q)] = (mid - inverse * two).astype(BF)


def compute(amps, ints, base, invd, am, im, rm):
    z, y = lax.axis_index("z"), lax.axis_index("y")
    xh, xl, c = lax.axis_index("xh"), lax.axis_index("xl"), lax.axis_index("c")
    place = (xh * 2 + xl) | (c << 2) | (z << 3) | (y << 6)
    idx = (am | (im << IMASK) | (rm << RMASK) | (place << 3)).astype(jnp.int32)

    cut = list(call(prep_w, [shape(512, 128)] * 4, [SM, VM], [VM] * 4)(idx, ints))
    for i in range(4):
        cut[i] = permute_x(cut[i], lambda h, l, k, i=i: (k ^ (i >> 1), l ^ (i & 1), h))
    own = [call(join_w, shape(1024, 128), [VM] * 2, VM)(cut[2 * a], cut[2 * a + 1]) for a in range(2)]

    masked = call(prep_a, shape(512, 512), [SM, VM], VM)(idx, amps)
    terms = call(prep_t, [shape(2, 512, 128)] * 4, [SM, VM, VM], [VM] * 4)(idx, base, invd)

    pieces = [[own[0]] + [None] * 7, [own[1]] + [None] * 7]
    up, down = list(own), list(own)
    for step in range(1, 4):
        for g in range(2):
            up[g] = shift_z(up[g], 1)
            down[g] = shift_z(down[g], -1)
            pieces[g][8 - step] = up[g]
            pieces[g][step] = down[g]
    pieces[0][4] = shift_z(up[0], 1)
    pieces[1][4] = shift_z(down[1], -1)

    left = [masked]
    for j in range(1, 4):
        left.append(chip_xor(masked, j))
    joined = call(join_a, shape(4, 512, 512), [VM] * 4, VM)(*left)
    left.append(core_swap(joined))
    terms = list(terms)
    for j in range(1, 4):
        terms[j] = chip_xor(terms[j], j)

    sends = first_product((0, 1), idx, pieces, left, [])
    sends = first_product((2,), idx, pieces, left, sends)
    sends = first_product((3,), idx, pieces, left, sends)
    w_all = call(arrange, shape(4, 2048, 256), [SM] + [VM] * 16, VM, moved=8 << 20)(idx, *pieces[0], *pieces[1])

    def reduced(sends):
        got = [sends[0]] + [None] * 3
        for t in (2, 1, 3):
            got[t] = xor_y(sends[t], t)
        return got

    def spread(values):
        got = [values[0]] + [None] * 3
        for j in (2, 1, 3):
            got[j] = chip_xor(values[j], j)
        return got

    nxt, *ladder = update(0, idx, reduced(sends), left[:4], terms, [])
    chips = spread([nxt] * 4)
    chips = chips + [core_swap(v) for v in chips]
    parts = [None] * 4
    for t in (2, 1, 3, 0):
        parts[t] = second_product(t, idx, chips, w_all)
    parts = reduced(parts)
    first = spread(ladder)
    ladder = call(sum_kernel, [shape(512, 128)] * 4, [SM] + [VM] * 4, [VM] * 4)(idx, *parts)
    second = spread(ladder)
    return call(
        final_kernel, [shape(512, 512), shape(512, 512, dtype=F32)], [SM] + [VM] * 11, [VM] * 2, moved=6 << 20
    )(idx, amps, base, invd, *first, *second)


def solution(mesh):
    split = Mesh(mesh.devices.reshape(8, 2, 4, 2, 2), ("z", "xh", "y", "xl", "c"))
    row, col = ("z", "xh"), ("y", "xl", "c")
    return jax.shard_map(
        compute,
        mesh=split,
        in_specs=(P(row, col), P(col, row), P(row, col), P(row, col), P(row, col), P(col, row), P(row, col)),
        out_specs=(P(row, col), P(row, col)),
        check_vma=False,
    )
```

```python
import functools

import jax
import jax.numpy as jnp
from jax import lax
from jax.experimental import pallas as pl
from jax.experimental.pallas import tpu as pltpu
from jax.sharding import Mesh
from jax.sharding import PartitionSpec as P

AX = ("xh", "xl", "c")
BF = jnp.bfloat16
F32 = jnp.float32
LIMIT = 24 << 20
VM = pl.BlockSpec(memory_space=pltpu.VMEM)
SM = pl.BlockSpec(memory_space=pltpu.SMEM)
ANY = pl.BlockSpec(memory_space=pl.ANY)


def shape(*dims, dtype=BF):
    return jax.ShapeDtypeStruct(dims, dtype)


def permute_x(value, move):
    pairs = []
    for xh in range(2):
        for xl in range(2):
            for c in range(2):
                th, tl, tc = move(xh, xl, c)
                pairs.append((xh * 4 + xl * 2 + c, th * 4 + tl * 2 + tc))
    return lax.ppermute(value, AX, pairs)


def chip_xor(value, j):
    return permute_x(value, lambda xh, xl, c: (xh ^ (j >> 1), xl ^ (j & 1), c))


def core_swap(value):
    return permute_x(value, lambda xh, xl, c: (xh, xl, 1 - c))


def swap_z(value, side):
    return lax.ppermute(value, "z", [(i, (((i - side) % 8 ^ 1) + side) % 8) for i in range(8)])


def xor_y(value, t):
    return lax.ppermute(value, "y", [(i, i ^ t) for i in range(4)])


def call(body, outs, in_specs, out_specs, flops=0, moved=1 << 20, **kw):
    return pl.pallas_call(
        body,
        out_shape=outs,
        in_specs=in_specs,
        out_specs=out_specs,
        cost_estimate=pl.CostEstimate(flops=flops, bytes_accessed=moved, transcendentals=0),
        compiler_params=pltpu.CompilerParams(vmem_limit_bytes=LIMIT),
        **kw,
    )


def kept(idx, which, r, s):
    return (idx[r, s] >> which) & 1


def placed(idx):
    place = idx[0, 0] >> 3
    return [(place >> at) & size for at, size in ((0, 3), (2, 1), (1, 1), (0, 1), (3, 7), (6, 3))]


AMASK, IMASK, RMASK = 0, 1, 2


def lanes(q):
    return pl.ds(pl.multiple_of(q * 128, 128), 128)


def prep_w(idx, ints, *outs):
    _, c, _, xl, _, _ = placed(idx)
    for a in range(2):
        for b in range(2):
            col = c ^ a
            for r in range(2):
                keep = kept(idx, IMASK, r, col).astype(BF)
                outs[a * 2 + b][r * 256 : r * 256 + 256] = ints[r * 256 : r * 256 + 256, lanes(col * 2 + (xl ^ b))] * keep


def join_w(low, high, out):
    out[:512] = low[...]
    out[512:] = high[...]


def join_a(zero, one, two, three, out):
    out[0] = zero[...]
    out[1] = one[...]
    out[2] = two[...]
    out[3] = three[...]


def prep_a(idx, amps, masked):
    for r in range(2):
        for s in range(2):
            tile = (slice(r * 256, r * 256 + 256), slice(s * 256, s * 256 + 256))
            masked[tile] = amps[tile] * kept(idx, AMASK, r, s).astype(BF)


def prep_t(idx, base, invd, *outs):
    d = placed(idx)[0]
    for r in range(2):
        rows = slice(r * 256, r * 256 + 256)
        for j in range(4):
            q = d ^ j
            keep = (kept(idx, AMASK, r, q >> 1) * kept(idx, RMASK, r, q >> 1)).astype(F32)
            outs[j][0, rows] = base[rows, lanes(q)].astype(BF)
            outs[j][1, rows] = (invd[rows, lanes(q)] * keep).astype(BF)


PAIRS = (((0, 0), (0, 1)), ((1, 2), (1, 1)), ((0, 2), (0, 3)), ((0, 4), (1, 3)))


def first_kernel(ks, count, idx, *refs):
    pairs = [refs[4 * i : 4 * i + 4] for i in range(len(ks))]
    refs = refs[4 * len(ks) :]
    left, rest = refs[:4], refs[4]
    sends, wv, outv, osem = (lambda r: (r[:4], *r[4:]))(refs[5 + count :])
    _, c, xh, _, z, y = placed(idx)
    odd_z = z & 1
    flip = c ^ xh
    dests = [(z // 2 + (0, 3 - odd_z * 2, 1 + odd_z * 2, 2)[k]) & 3 for k in ks]

    def store(i, t):
        return pltpu.make_async_copy(outv.at[i], sends[t], osem.at[i])

    for i in range(len(ks)):
        for at in range(2):
            for a in range(2):
                wv[a, :, lanes(at ^ odd_z)] = pairs[i][at * 2 + a][...]

        @pl.loop(0, 2)
        def _(r, i=i):
            rows = pl.ds(pl.multiple_of(r * 256, 256), 256)
            for half in range(2):
                own = jnp.concatenate([left[half * 2][rows], left[half * 2 + 1][rows]], 1)
                other = jnp.concatenate([rest[half * 2, rows], rest[half * 2 + 1, rows]], 1)
                total = jnp.dot(own, wv[flip], preferred_element_type=F32)
                total += jnp.dot(other, wv[1 - flip], preferred_element_type=F32)
                outv[i, xh ^ half, rows] = total.astype(BF)

        for t in range(4):

            @pl.when((dests[i] ^ y) == t)
            def _(i=i, t=t):
                store(i, t).start()

    for i in range(len(ks)):
        store(i, 0).wait()


def first_product(ks, idx, pieces, left, carried):
    group = [pieces[a][at] for k in ks for at in PAIRS[k] for a in range(2)]
    return call(
        functools.partial(first_kernel, ks, len(carried)),
        [shape(2, 512, 256)] * 4,
        [SM] + [VM] * len(group) + [VM] * 5 + [ANY] * len(carried),
        [ANY] * 4,
        flops=len(ks) * 2 * 1024 * 2048 * 256,
        moved=len(ks) << 20,
        scratch_shapes=[
            pltpu.VMEM((2, 1024, 256), BF),
            pltpu.VMEM((len(ks), 2, 512, 256), BF),
            pltpu.SemaphoreType.DMA((len(ks),)),
        ],
        input_output_aliases={6 + len(group) + i: i for i in range(len(carried))},
    )(idx, *group, *left, *carried)


ORDER = tuple(at for pair in PAIRS for at in pair)


def arrange(idx, *refs):
    d, c, xh, xl, z, _ = placed(idx)
    out = refs[16]
    up = 1 - 2 * (z & 1)
    for a in range(2):
        for s, (side, step) in enumerate(ORDER):
            piece = refs[a * 8 + s]
            owner = (z + (1 - 2 * side) * step * up) & 7

            @pl.loop(0, 8)
            def _(block, a=a, piece=piece, owner=owner):
                e, q = block >> 2, block & 3
                at = (((a ^ c ^ xh) * 4 + (q ^ d)) * 2 + (e ^ xl)) * 128
                rows = pl.ds(pl.multiple_of(at, 128), 128)
                out[owner >> 1, rows, lanes(owner & 1)] = piece[pl.ds(pl.multiple_of(block * 128, 128), 128)]


def join_b(one, two, three, out):
    out[0] = one[...]
    out[1] = two[...]
    out[2] = three[...]


def second_kernel(idx, *refs):
    own, swapped, joined, weights, out = refs[:4], refs[4], refs[5], refs[6], refs[7]
    left = [ref[...] for ref in own] + [swapped[...]] + [joined[i] for i in range(3)]
    left = jnp.concatenate([v.reshape(512, 256) for v in left], 1)
    out[...] = jnp.dot(left, weights[...], preferred_element_type=F32).astype(BF).reshape(2, 256, 256)


def second_product(t, idx, left, w_all):
    whole = pl.BlockSpec((2, 256, 256), lambda i, s: (0, 0, 0))
    return pl.pallas_call(
        second_kernel,
        out_shape=shape(2, 256, 256),
        grid_spec=pltpu.PrefetchScalarGridSpec(
            num_scalar_prefetch=1,
            grid=(1,),
            in_specs=[whole] * 5
            + [
                pl.BlockSpec((3, 2, 256, 256), lambda i, s: (0, 0, 0, 0)),
                pl.BlockSpec((None, 2048, 256), lambda i, s: (placed(s)[5] ^ t, 0, 0)),
            ],
            out_specs=whole,
        ),
        name="second",
        compiler_params=pltpu.CompilerParams(vmem_limit_bytes=LIMIT),
        cost_estimate=pl.CostEstimate(flops=2 * 512 * 2048 * 256, bytes_accessed=2 << 20, transcendentals=0),
    )(idx, *left, w_all)


def summed(parts, h, e, rows):
    total = parts[0][h, rows, lanes(e)].astype(F32)
    for part in parts[1:]:
        total += part[h, rows, lanes(e)].astype(F32)
    return total


def update_kernel(idx, *refs):
    parts, left, terms, nxt, outs = refs[:4], refs[4:8], refs[8:12], refs[12:14], refs[14:]
    d = placed(idx)[0]

    for n in range(2):

        @pl.loop(0, 2)
        def _(i, n=n):
            rows = lanes(2 * n + i)
            for j in range(4):
                h, e = (d ^ j) >> 1, (d ^ j) & 1
                ladder = summed(parts, h, e, rows)
                outs[j][rows] = ladder.astype(BF)
                step = terms[j][1, rows].astype(F32) * (terms[j][0, rows].astype(F32) + ladder)
                nxt[n][h, lanes(i), lanes(e)] = (left[j][rows].astype(F32) - step).astype(BF)


def update(idx, parts, left, terms):
    whole = pl.BlockSpec((2, 512, 256), lambda i, s: (0, 0, 0))
    half = pl.BlockSpec((2, 256, 256), lambda i, s: (0, 0, 0))
    quarter = pl.BlockSpec((512, 128), lambda i, s: (0, 0))
    return pl.pallas_call(
        update_kernel,
        out_shape=[shape(2, 256, 256)] * 2 + [shape(512, 128)] * 4,
        grid_spec=pltpu.PrefetchScalarGridSpec(
            num_scalar_prefetch=1,
            grid=(1,),
            in_specs=[whole] * 4
            + [pl.BlockSpec((512, 128), lambda i, s: (0, placed(s)[0]))] * 4
            + [pl.BlockSpec((2, 512, 128), lambda i, s: (0, 0, 0))] * 4,
            out_specs=[half] * 2 + [quarter] * 4,
        ),
        name="update",
        compiler_params=pltpu.CompilerParams(vmem_limit_bytes=LIMIT),
        cost_estimate=pl.CostEstimate(flops=0, bytes_accessed=2 << 20, transcendentals=0),
    )(idx, *parts, *left, *terms)


def sum_kernel(idx, *refs):
    parts, outs = refs[:-4], refs[-4:]
    d = placed(idx)[0]
    for n in range(2):

        @pl.loop(0, 2)
        def _(i, n=n):
            for j in range(4):
                ladder = summed(parts[n * 4 : n * 4 + 4], (d ^ j) >> 1, (d ^ j) & 1, lanes(i))
                outs[j][lanes(2 * n + i)] = ladder.astype(BF)


def final_kernel(idx, amps, base, invd, *refs):
    first, second, new, res = refs[:4], refs[4:8], refs[-2], refs[-1]
    d = placed(idx)[0]

    @pl.loop(0, 4)
    def _(i):
        rows = lanes(i)
        for j in range(4):
            q = d ^ j
            keep = kept(idx, RMASK, i >> 1, q >> 1).astype(F32)
            fixed, inverse = base[rows, lanes(q)], invd[rows, lanes(q)]
            one = (fixed + first[j][rows].astype(F32)) * keep
            mid = (amps[rows, lanes(q)].astype(F32) - inverse * one).astype(BF).astype(F32)
            two = (fixed + second[j][rows].astype(F32)) * keep
            res[rows, lanes(q)] = two
            new[rows, lanes(q)] = (mid - inverse * two).astype(BF)


def compute(amps, ints, base, invd, am, im, rm):
    z, y = lax.axis_index("z"), lax.axis_index("y")
    xh, xl, c = lax.axis_index("xh"), lax.axis_index("xl"), lax.axis_index("c")
    place = (xh * 2 + xl) | (c << 2) | (z << 3) | (y << 6)
    idx = (am | (im << IMASK) | (rm << RMASK) | (place << 3)).astype(jnp.int32)

    cut = list(call(prep_w, [shape(512, 128)] * 4, [SM, VM], [VM] * 4)(idx, ints))
    for i in range(4):
        cut[i] = permute_x(cut[i], lambda h, l, k, i=i: (k ^ (i >> 1), l ^ (i & 1), h))
    own = [call(join_w, shape(1024, 128), [VM] * 2, VM)(cut[2 * a], cut[2 * a + 1]) for a in range(2)]

    masked = call(prep_a, shape(512, 512), [SM, VM], VM)(idx, amps)
    terms = call(prep_t, [shape(2, 512, 128)] * 4, [SM, VM, VM], [VM] * 4)(idx, base, invd)

    pieces = [{(0, 0): own[g]} for g in range(2)]
    sent = [[v, v] for v in own]
    for step in range(1, 4):
        for g in range(2):
            for side in range(2):
                pieces[g][side, step] = swap_z(sent[g][side], side)
            sent[g] = [pieces[g][1, step], pieces[g][0, step]]
    pieces[0][0, 4] = swap_z(sent[0][0], 0)
    pieces[1][0, 4] = swap_z(sent[1][1], 1)

    left = [masked]
    for j in range(1, 4):
        left.append(chip_xor(masked, j))
    joined = call(join_a, shape(4, 512, 512), [VM] * 4, VM)(*left)
    left.append(core_swap(joined))
    terms = list(terms)
    for j in range(1, 4):
        terms[j] = chip_xor(terms[j], j)

    sends = first_product((0, 1), idx, pieces, left, [])
    sends = first_product((2,), idx, pieces, left, sends)
    sends = first_product((3,), idx, pieces, left, sends)
    w_all = call(arrange, shape(4, 2048, 256), [SM] + [VM] * 16, VM, moved=8 << 20)(
        idx, *(pieces[g][at] for g in range(2) for at in ORDER)
    )

    def reduced(sends):
        got = [sends[0]] + [None] * 3
        for t in (2, 1, 3):
            got[t] = xor_y(sends[t], t)
        return got

    def spread(values):
        got = [values[0]] + [None] * 3
        for j in (2, 1, 3):
            got[j] = chip_xor(values[j], j)
        return got

    *nxt, l0, l1, l2, l3 = update(idx, reduced(sends), left[:4], terms)
    first = spread([l0, l1, l2, l3])
    parts = []
    for n in range(2):
        chips = spread([nxt[n]] * 4)
        chips.append(core_swap(nxt[n]))
        joined = call(join_b, shape(3, 2, 256, 256), [VM] * 3, VM)(*chips[1:4])
        chips.append(core_swap(joined))
        got = [None] * 4
        for t in (2, 1, 3, 0):
            got[t] = second_product(t, idx, chips, w_all)
        parts += reduced(got)
    ladder = call(sum_kernel, [shape(512, 128)] * 4, [SM] + [VM] * 8, [VM] * 4)(idx, *parts)
    second = spread(ladder)
    return call(
        final_kernel, [shape(512, 512), shape(512, 512, dtype=F32)], [SM] + [VM] * 11, [VM] * 2, moved=6 << 20
    )(idx, amps, base, invd, *first, *second)


def solution(mesh):
    split = Mesh(mesh.devices.reshape(8, 2, 4, 2, 2), ("z", "xh", "y", "xl", "c"))
    row, col = ("z", "xh"), ("y", "xl", "c")
    return jax.shard_map(
        compute,
        mesh=split,
        in_specs=(P(row, col), P(col, row), P(row, col), P(row, col), P(row, col), P(col, row), P(row, col)),
        out_specs=(P(row, col), P(row, col)),
        check_vma=False,
    )
```

```python
import functools

import jax
import jax.numpy as jnp
from jax import lax
from jax.experimental import pallas as pl
from jax.experimental.pallas import tpu as pltpu
from jax.sharding import Mesh
from jax.sharding import PartitionSpec as P

AX = ("xh", "xl", "c")
BF = jnp.bfloat16
F32 = jnp.float32
LIMIT = 24 << 20
VM = pl.BlockSpec(memory_space=pltpu.VMEM)
SM = pl.BlockSpec(memory_space=pltpu.SMEM)
ANY = pl.BlockSpec(memory_space=pl.ANY)


def shape(*dims, dtype=BF):
    return jax.ShapeDtypeStruct(dims, dtype)


def permute_x(value, move):
    pairs = []
    for xh in range(2):
        for xl in range(2):
            for c in range(2):
                th, tl, tc = move(xh, xl, c)
                pairs.append((xh * 4 + xl * 2 + c, th * 4 + tl * 2 + tc))
    return lax.ppermute(value, AX, pairs)


def chip_xor(value, j):
    return permute_x(value, lambda xh, xl, c: (xh ^ (j >> 1), xl ^ (j & 1), c))


def core_swap(value):
    return permute_x(value, lambda xh, xl, c: (xh, xl, 1 - c))


def swap_z(value, side):
    return lax.ppermute(value, "z", [(i, (((i - side) % 8 ^ 1) + side) % 8) for i in range(8)])


def xor_y(value, t):
    return lax.ppermute(value, "y", [(i, i ^ t) for i in range(4)])


def call(body, outs, in_specs, out_specs, flops=0, moved=1 << 20, **kw):
    return pl.pallas_call(
        body,
        out_shape=outs,
        in_specs=in_specs,
        out_specs=out_specs,
        cost_estimate=pl.CostEstimate(flops=flops, bytes_accessed=moved, transcendentals=0),
        compiler_params=pltpu.CompilerParams(vmem_limit_bytes=LIMIT),
        **kw,
    )


def kept(idx, which, r, s):
    return (idx[r, s] >> which) & 1


def placed(idx):
    place = idx[0, 0] >> 3
    return [(place >> at) & size for at, size in ((0, 3), (2, 1), (1, 1), (0, 1), (3, 7), (6, 3))]


AMASK, IMASK, RMASK = 0, 1, 2


def lanes(q):
    return pl.ds(pl.multiple_of(q * 128, 128), 128)


def prep_w(idx, ints, *outs):
    _, c, _, xl, _, _ = placed(idx)
    for a in range(2):
        for b in range(2):
            col = c ^ a
            for r in range(2):
                keep = kept(idx, IMASK, r, col).astype(BF)
                outs[a * 2 + b][r * 256 : r * 256 + 256] = ints[r * 256 : r * 256 + 256, lanes(col * 2 + (xl ^ b))] * keep


def join_w(low, high, out):
    out[:512] = low[...]
    out[512:] = high[...]


def join_a(zero, one, two, three, out):
    @pl.loop(0, 4)
    def _(i):
        for j, ref in enumerate((zero, one, two, three)):
            out[j, lanes(i)] = ref[lanes(i)]


def prep_a(idx, amps, masked):
    for r in range(2):
        for s in range(2):
            tile = (slice(r * 256, r * 256 + 256), slice(s * 256, s * 256 + 256))
            masked[tile] = amps[tile] * kept(idx, AMASK, r, s).astype(BF)


def prep_t(idx, base, invd, *outs):
    d = placed(idx)[0]

    @pl.loop(0, 4)
    def _(i):
        rows = lanes(i)
        for j in range(4):
            q = d ^ j
            keep = (kept(idx, AMASK, i >> 1, q >> 1) * kept(idx, RMASK, i >> 1, q >> 1)).astype(F32)
            outs[j][0, rows] = base[rows, lanes(q)].astype(BF)
            outs[j][1, rows] = (invd[rows, lanes(q)] * keep).astype(BF)


PAIRS = (((0, 0), (0, 1)), ((1, 2), (1, 1)), ((0, 2), (0, 3)), ((0, 4), (1, 3)))


def first_kernel(ks, count, idx, *refs):
    pairs = [refs[4 * i : 4 * i + 4] for i in range(len(ks))]
    refs = refs[4 * len(ks) :]
    left, rest = refs[:4], refs[4]
    sends, wv, outv, osem = (lambda r: (r[:8], *r[8:]))(refs[5 + count :])
    _, c, xh, _, z, y = placed(idx)
    odd_z = z & 1
    flip = c ^ xh
    dests = [(z // 2 + (0, 3 - odd_z * 2, 1 + odd_z * 2, 2)[k]) & 3 for k in ks]

    def store(i, t, n):
        return pltpu.make_async_copy(outv.at[i, :, pl.ds(n * 256, 256)], sends[t * 2 + n], osem.at[i, n])

    for i in range(len(ks)):
        @pl.loop(0, 4)
        def _(r, i=i):
            rows = pl.ds(pl.multiple_of(r * 256, 256), 256)
            for at in range(2):
                for a in range(2):
                    wv[a, rows, lanes(at ^ odd_z)] = pairs[i][at * 2 + a][rows]

        @pl.loop(0, 2)
        def _(r, i=i):
            rows = pl.ds(pl.multiple_of(r * 256, 256), 256)
            for half in range(2):
                own = jnp.concatenate([left[half * 2][rows], left[half * 2 + 1][rows]], 1)
                other = jnp.concatenate([rest[half * 2, rows], rest[half * 2 + 1, rows]], 1)
                total = jnp.dot(own, wv[flip], preferred_element_type=F32)
                total += jnp.dot(other, wv[1 - flip], preferred_element_type=F32)
                outv[i, xh ^ half, rows] = total.astype(BF)

        for t in range(4):

            @pl.when((dests[i] ^ y) == t)
            def _(i=i, t=t):
                store(i, t, 0).start()
                store(i, t, 1).start()

    for i in range(len(ks)):
        store(i, 0, 0).wait()
        store(i, 0, 1).wait()


def first_product(ks, idx, pieces, left, carried):
    group = [pieces[a][at] for k in ks for at in PAIRS[k] for a in range(2)]
    return call(
        functools.partial(first_kernel, ks, len(carried)),
        [shape(2, 256, 256)] * 8,
        [SM] + [VM] * len(group) + [VM] * 5 + [ANY] * len(carried),
        [ANY] * 8,
        flops=len(ks) * 2 * 1024 * 2048 * 256,
        moved=len(ks) << 20,
        scratch_shapes=[
            pltpu.VMEM((2, 1024, 256), BF),
            pltpu.VMEM((len(ks), 2, 512, 256), BF),
            pltpu.SemaphoreType.DMA((len(ks), 2)),
        ],
        input_output_aliases={6 + len(group) + i: i for i in range(len(carried))},
    )(idx, *group, *left, *carried)


ORDER = tuple(at for pair in PAIRS for at in pair)


def arrange(idx, *refs):
    d, c, xh, xl, z, _ = placed(idx)
    out = refs[16]
    up = 1 - 2 * (z & 1)
    for a in range(2):
        for s, (side, step) in enumerate(ORDER):
            piece = refs[a * 8 + s]
            owner = (z + (1 - 2 * side) * step * up) & 7

            @pl.loop(0, 8)
            def _(block, a=a, piece=piece, owner=owner):
                e, q = block >> 2, block & 3
                at = (((a ^ c ^ xh) * 4 + (q ^ d)) * 2 + (e ^ xl)) * 128
                rows = pl.ds(pl.multiple_of(at, 128), 128)
                out[owner >> 1, rows, lanes(owner & 1)] = piece[pl.ds(pl.multiple_of(block * 128, 128), 128)]


def join_b(zero, one, two, three, out):
    out[0] = zero[...]
    out[1] = one[...]
    out[2] = two[...]
    out[3] = three[...]


def second_kernel(idx, *refs):
    own, swapped, weights, out = refs[:4], refs[4], refs[5], refs[6]
    left = [ref[...] for ref in own] + [swapped[i] for i in range(4)]
    left = jnp.concatenate([v.reshape(512, 256) for v in left], 1)
    out[...] = jnp.dot(left, weights[...], preferred_element_type=F32).astype(BF).reshape(2, 256, 256)


def second_product(t, idx, left, w_all):
    whole = pl.BlockSpec((2, 256, 256), lambda i, s: (0, 0, 0))
    return pl.pallas_call(
        second_kernel,
        out_shape=shape(2, 256, 256),
        grid_spec=pltpu.PrefetchScalarGridSpec(
            num_scalar_prefetch=1,
            grid=(1,),
            in_specs=[whole] * 4
            + [
                pl.BlockSpec((4, 2, 256, 256), lambda i, s: (0, 0, 0, 0)),
                pl.BlockSpec((None, 2048, 256), lambda i, s: (placed(s)[5] ^ t, 0, 0)),
            ],
            out_specs=whole,
        ),
        name="second",
        compiler_params=pltpu.CompilerParams(vmem_limit_bytes=LIMIT),
        cost_estimate=pl.CostEstimate(flops=2 * 512 * 2048 * 256, bytes_accessed=2 << 20, transcendentals=0),
    )(idx, *left, w_all)


def summed(parts, h, e, rows):
    total = parts[0][h, rows, lanes(e)].astype(F32)
    for part in parts[1:]:
        total += part[h, rows, lanes(e)].astype(F32)
    return total


def update_kernel(n, idx, *refs):
    parts, left, terms, nxt, outs = refs[:4], refs[4:8], refs[8:12], refs[12], refs[13:]
    d = placed(idx)[0]

    @pl.loop(0, 2)
    def _(i):
        here, rows = lanes(i), lanes(2 * n + i)
        for j in range(4):
            h, e = (d ^ j) >> 1, (d ^ j) & 1
            ladder = summed(parts, h, e, here)
            outs[j][here] = ladder.astype(BF)
            step = terms[j][1, rows].astype(F32) * (terms[j][0, rows].astype(F32) + ladder)
            nxt[h, here, lanes(e)] = (left[j][rows, lanes(d)].astype(F32) - step).astype(BF)


def update(n, idx, parts, left, terms):
    return call(
        functools.partial(update_kernel, n),
        [shape(2, 256, 256)] + [shape(256, 128)] * 4,
        [SM] + [VM] * 12,
        [VM] * 5,
        moved=3 << 20,
    )(idx, *parts, *left, *terms)


def join_e(*refs):
    for j in range(4):
        refs[8 + j][:256] = refs[j][...]
        refs[8 + j][256:] = refs[4 + j][...]


def sum_kernel(idx, *refs):
    parts, outs = refs[:-4], refs[-4:]
    d = placed(idx)[0]
    for n in range(2):

        @pl.loop(0, 2)
        def _(i, n=n):
            for j in range(4):
                ladder = summed(parts[n * 4 : n * 4 + 4], (d ^ j) >> 1, (d ^ j) & 1, lanes(i))
                outs[j][lanes(2 * n + i)] = ladder.astype(BF)


def final_kernel(idx, amps, base, invd, *refs):
    first, second, new, res = refs[:4], refs[4:8], refs[-2], refs[-1]
    d = placed(idx)[0]

    @pl.loop(0, 4)
    def _(i):
        rows = lanes(i)
        for j in range(4):
            q = d ^ j
            keep = kept(idx, RMASK, i >> 1, q >> 1).astype(F32)
            fixed, inverse = base[rows, lanes(q)], invd[rows, lanes(q)]
            one = (fixed + first[j][rows].astype(F32)) * keep
            mid = (amps[rows, lanes(q)].astype(F32) - inverse * one).astype(BF).astype(F32)
            two = (fixed + second[j][rows].astype(F32)) * keep
            res[rows, lanes(q)] = two
            new[rows, lanes(q)] = (mid - inverse * two).astype(BF)


def compute(amps, ints, base, invd, am, im, rm):
    z, y = lax.axis_index("z"), lax.axis_index("y")
    xh, xl, c = lax.axis_index("xh"), lax.axis_index("xl"), lax.axis_index("c")
    place = (xh * 2 + xl) | (c << 2) | (z << 3) | (y << 6)
    idx = (am | (im << IMASK) | (rm << RMASK) | (place << 3)).astype(jnp.int32)

    cut = list(call(prep_w, [shape(512, 128)] * 4, [SM, VM], [VM] * 4)(idx, ints))
    for i in range(4):
        cut[i] = permute_x(cut[i], lambda h, l, k, i=i: (k ^ (i >> 1), l ^ (i & 1), h))
    own = [call(join_w, shape(1024, 128), [VM] * 2, VM)(cut[2 * a], cut[2 * a + 1]) for a in range(2)]

    masked = call(prep_a, shape(512, 512), [SM, VM], VM)(idx, amps)
    terms = call(prep_t, [shape(2, 512, 128)] * 4, [SM, VM, VM], [VM] * 4)(idx, base, invd)

    pieces = [{(0, 0): own[g]} for g in range(2)]
    sent = [[v, v] for v in own]
    for step in range(1, 4):
        for g in range(2):
            for side in range(2):
                pieces[g][side, step] = swap_z(sent[g][side], side)
            sent[g] = [pieces[g][1, step], pieces[g][0, step]]
    pieces[0][0, 4] = swap_z(sent[0][0], 0)
    pieces[1][0, 4] = swap_z(sent[1][1], 1)

    left = [masked]
    for j in range(1, 4):
        left.append(chip_xor(masked, j))
    joined = call(join_a, shape(4, 512, 512), [VM] * 4, VM)(*left)
    left.append(core_swap(joined))
    terms = list(terms)
    for j in range(1, 4):
        terms[j] = chip_xor(terms[j], j)

    sends = first_product((0, 1), idx, pieces, left, [])
    sends = first_product((2,), idx, pieces, left, sends)
    sends = first_product((3,), idx, pieces, left, sends)
    w_all = call(arrange, shape(4, 2048, 256), [SM] + [VM] * 16, VM, moved=8 << 20)(
        idx, *(pieces[g][at] for g in range(2) for at in ORDER)
    )

    def reduced(sends):
        got = [sends[0]] + [None] * 3
        for t in (2, 1, 3):
            got[t] = xor_y(sends[t], t)
        return got

    def spread(values):
        got = [values[0]] + [None] * 3
        for j in (2, 1, 3):
            got[j] = chip_xor(values[j], j)
        return got

    nxt, ladder = [None] * 2, []
    for n in range(2):
        parts = reduced(sends[n::2])
        nxt[n], *out = update(n, idx, parts, left[:4], terms)
        ladder += out
    ladder = call(join_e, [shape(512, 128)] * 4, [VM] * 8, [VM] * 4)(*ladder)
    first = spread(ladder)
    parts = []
    for n in range(2):
        chips = spread([nxt[n]] * 4)
        joined = call(join_b, shape(4, 2, 256, 256), [VM] * 4, VM)(*chips)
        chips.append(core_swap(joined))
        got = [None] * 4
        for t in (2, 1, 3, 0):
            got[t] = second_product(t, idx, chips, w_all)
        parts += reduced(got)
    ladder = call(sum_kernel, [shape(512, 128)] * 4, [SM] + [VM] * 8, [VM] * 4)(idx, *parts)
    second = spread(ladder)
    return call(
        final_kernel, [shape(512, 512), shape(512, 512, dtype=F32)], [SM] + [VM] * 11, [VM] * 2, moved=6 << 20
    )(idx, amps, base, invd, *first, *second)


def solution(mesh):
    split = Mesh(mesh.devices.reshape(8, 2, 4, 2, 2), ("z", "xh", "y", "xl", "c"))
    row, col = ("z", "xh"), ("y", "xl", "c")
    return jax.shard_map(
        compute,
        mesh=split,
        in_specs=(P(row, col), P(col, row), P(row, col), P(row, col), P(row, col), P(col, row), P(row, col)),
        out_specs=(P(row, col), P(row, col)),
        check_vma=False,
    )
```
